32 devices in a mesh: key: 4 (over x, core), head: 4 (over z), batch: 2 (over y).
Axes of the slice: x: 2, y: 2, z: 4, core: 2. Of those that a mesh axis runs over, the one named last changes fastest.
Arguments:
- new_queries: bfloat16 [16, 4, 4, 1024], P('batch', 'head'), parts along dimension 0, may hold values from -6 to 6
- new_keys: bfloat16 [16, 4, 4, 1024], P('batch', 'head'), parts along dimension 0, may hold values from -0.8984375 to 0.8984375
- new_values: bfloat16 [16, 4, 4, 1024], P('batch', 'head'), parts along dimension 0, may hold values from -6 to 6
- decay_gate: float32 [16, 4, 4], P('batch', 'head'), parts along dimension 0, may hold values from 0.85 to 0.999
- write_gate: float32 [16, 4, 4], P('batch', 'head'), parts along dimension 0, may hold values from 0.2 to 1
- ridge_shift: float32 [4], P('head'), may hold values from 0.5 to 2
- norm_gain: float32 [4, 1024], P('head', 'key'), may hold values from 0.1 to 1.9
- cov_state: bfloat16 [16, 4, 1024, 1024], P('batch', 'head', 'key'), parts along dimension 0, may hold values from -1 to 42, as said below
- value_state: bfloat16 [16, 4, 1024, 1024], P('batch', 'head', None, 'key'), parts along dimension 0, may hold values from -0.1875 to 0.1875
- out_weight: bfloat16 [4, 1024, 8192], P('head', 'key'), may hold values from -0.125 to 0.125
Outputs:
- layer_out: bfloat16 [16, 4, 8192], P('batch', None, ('key', 'head')), parts along dimension 0
The draws below stay inside these ranges and needn't reach their ends.
There are 2 independent parts, one for each index of `batch`. The reference program is written for one: setup_inputs(seed, part) draws one part's arguments, and reference() takes and returns one part's arrays. A program takes and returns all parts, laid end to end along the dimension named above; an argument that names none is the same for every part. Nothing has to cross between parts.
Inputs may be any that keep to these rules, and one draw needn't show every extreme that they name: `cov_state`: each 1024 x 1024 block is symmetric and positive definite.
All inputs are finite; a program needn't handle non-finite values.
Results may differ from the reference program's by a relative error of at most 0.0085.
Values may be sent and summed in bfloat16 or wider, within the bound.
A program may use at most 64 MiB of HBM per device.

```python
import math
import jax
import jax.numpy as jnp
from jax import lax

DK = 1024
DV = 1024
DM = 8192
SEQS = 8
DRAFT = 4
ITERS = 3
HEADS = 4


def draw_cov_state(key, part):
    first_key, second_key = jax.random.split(jax.random.fold_in(key, 17))
    log_diag = jax.random.uniform(first_key, (SEQS, HEADS, DK), jnp.float32, math.log(2.0), math.log(20.0))
    noise = jax.random.normal(second_key, (SEQS, HEADS, DK, DK), jnp.float32)
    symmetric = (noise + jnp.swapaxes(noise, 2, 3)) * (0.02 / math.sqrt(2.0))
    diagonal = jnp.exp(log_diag)[..., None] * jnp.eye(DK, dtype=jnp.float32)
    return (symmetric + diagonal).astype(jnp.bfloat16)


def with_spikes(values, rng, source, target, blocks, factor):
    def block_of(axis_at):
        return (jnp.arange(values.shape[axis_at]) // (values.shape[axis_at] // blocks)).reshape((-1,) + (1,) * (values.ndim - 1 - axis_at))

    near = jax.random.permutation(rng, blocks)[block_of(target)]
    other_side = (block_of(target) + blocks // 2) % blocks
    return jnp.where((block_of(source) == near) | (block_of(source) == other_side), factor * values, values)


def block_levels(key, dims, cuts, least, largest):
    gain = 1.0
    for dim, blocks in cuts:
        draws = jax.random.uniform(jax.random.fold_in(jax.random.fold_in(key, 6), dim), (blocks,), jnp.float32, least / len(cuts), largest / len(cuts))
        gain = gain * jnp.repeat(jnp.exp(draws), dims[dim] // blocks).reshape((-1,) + (1,) * (len(dims) - 1 - dim))
    return gain


def bell_draw(rng, extent, deviation, most, cuts=(), held_as=jnp.bfloat16):
    gain = block_levels(rng, extent, cuts, -0.22, 0.18) if cuts else 1.0
    entries = jax.random.normal(rng, extent, jnp.float32) * deviation * gain
    return jnp.minimum(jnp.maximum(entries, -most), most).astype(held_as)


def heavy_noise(key, dims, spread, limit, shards, heavy, held_as=jnp.bfloat16):
    drawn = spread * jax.random.normal(key, dims, jnp.float32)
    if shards:
        drawn = drawn * block_levels(key, dims, shards, -0.22, 0.18)
    return jnp.clip(with_spikes(drawn, jax.random.fold_in(key, 3), *heavy), -limit, limit).astype(held_as)


def setup_inputs(seed: int = 0, part: int = 0) -> dict:
    streams_of = jax.random.split(jax.random.key(seed), 11)
    own_keys = jax.random.split(jax.random.fold_in(streams_of[10], part), 11)
    return {
        "new_queries": bell_draw(own_keys[0], (SEQS, HEADS, DRAFT, DK), 1.0, 6.0, ((1, 4),)),
        "new_keys": bell_draw(own_keys[1], (SEQS, HEADS, DRAFT, DK), 0.15, 0.8984375, ((1, 4),)),
        "new_values": bell_draw(own_keys[2], (SEQS, HEADS, DRAFT, DV), 1.0, 6.0, ((1, 4),)),
        "decay_gate": jnp.clip(jnp.exp(math.log(0.999) - 0.16151841 * jax.random.uniform(own_keys[3], (SEQS, HEADS, DRAFT), jnp.float32) ** block_levels(own_keys[3], (SEQS, HEADS, DRAFT), ((1, 4),), -0.2, 0.2)), 0.85, 0.999),
        "write_gate": jnp.clip(0.2 + 0.8 * jax.random.uniform(own_keys[4], (SEQS, HEADS, DRAFT), jnp.float32) ** block_levels(own_keys[4], (SEQS, HEADS, DRAFT), ((1, 4),), -0.2, 0.2), 0.2, 1.0),
        "ridge_shift": jnp.clip(jnp.exp(math.log(2.0) - 1.3862944 * jax.random.uniform(streams_of[5], (HEADS,), jnp.float32) ** block_levels(streams_of[5], (HEADS,), ((0, 4),), -0.2, 0.2)), 0.5, 2.0),
        "norm_gain": jnp.clip(1.0 + 0.18 * jax.random.normal(streams_of[6], (HEADS, DV), jnp.float32), 0.1, 1.9),
        "cov_state": draw_cov_state(jax.random.fold_in(jax.random.fold_in(streams_of[10], part), 71), part),
        "value_state": bell_draw(own_keys[8], (SEQS, HEADS, DV, DK), DK ** -0.5, 0.1875, ((1, 4), (3, 4))),
        "out_weight": heavy_noise(streams_of[9], (HEADS, DV, DM), (HEADS * DV) ** -0.5, 0.125, ((0, 4), (1, 4)), (0, 2, 4, 2.0)),
    }


def coefficients(decay_gate, write_gate):
    decay_total = jnp.cumprod(decay_gate, axis=-1)
    decay_ratio = decay_total[..., :, None] / decay_total[..., None, :]
    is_later = jnp.arange(DRAFT)[:, None] >= jnp.arange(DRAFT)[None, :]
    mix_weights = jnp.where(is_later, write_gate[..., None, :] * decay_ratio, jnp.zeros_like(decay_ratio))
    return (decay_total, mix_weights)

def to_bf16_f32(vector):
    rounded = lax.optimization_barrier(vector.astype(jnp.bfloat16))
    return rounded.astype(jnp.float32)

def reference(new_queries, new_keys, new_values, decay_gate, write_gate, ridge_shift, norm_gain, cov_state, value_state, out_weight):
    high = lax.Precision.HIGHEST
    decay_total, mix_weights = coefficients(decay_gate, write_gate)
    keys_f = new_keys.astype(jnp.float32)
    values_f = new_values.astype(jnp.float32)
    cov_f = cov_state.astype(jnp.float32)
    ridge_term = ridge_shift[None, :, None, None]

    def operator(vector):
        vec_b = to_bf16_f32(vector)
        state_prod = jnp.einsum('shic,shtc->shti', cov_f, vec_b, precision=high)
        key_dots = jnp.einsum('shtc,shuc->shtu', vec_b, keys_f, precision=high)
        low_rank = jnp.einsum('shtu,shuc->shtc', mix_weights * key_dots, keys_f, precision=high)
        return decay_total[..., None] * state_prod + low_rank + ridge_term * vector
    residual = new_queries.astype(jnp.float32)
    direction = residual
    solution = jnp.zeros_like(residual)
    sq_norm = lax.optimization_barrier(jnp.sum(residual * residual, axis=-1))
    for sweep_index in range(ITERS):
        applied = operator(direction)
        step_size = sq_norm / lax.optimization_barrier(jnp.sum(direction * applied, axis=-1))
        solution = solution + step_size[..., None] * direction
        residual = residual - step_size[..., None] * applied
        new_norm = lax.optimization_barrier(jnp.sum(residual * residual, axis=-1))
        direction = residual + (new_norm / sq_norm)[..., None] * direction
        sq_norm = new_norm
    sol_b = to_bf16_f32(solution)
    state_read = jnp.einsum('shvc,shtc->shtv', value_state.astype(jnp.float32), sol_b, precision=high)
    key_sol = jnp.einsum('shtc,shuc->shtu', sol_b, keys_f, precision=high)
    readout = decay_total[..., None] * state_read + jnp.einsum('shtu,shuv->shtv', mix_weights * key_sol, values_f, precision=high)
    mean_sq = lax.optimization_barrier(jnp.mean(readout * readout, axis=-1))
    normed = (readout * lax.rsqrt(mean_sq + 1e-06)[..., None] * norm_gain[None, :, None, :]).astype(jnp.bfloat16)
    result = jnp.einsum('shtv,hvm->stm', normed.astype(jnp.float32), out_weight.astype(jnp.float32), precision=high)
    return result.astype(jnp.bfloat16)
```

```python
import functools

import jax
import jax.numpy as jnp
from jax import lax
from jax.experimental import pallas as pl
from jax.experimental.pallas import tpu as pltpu
from jax.sharding import PartitionSpec as P

ITERS = 3
MESH = pl.DeviceIdType.MESH
F32 = jnp.float32
BF16 = jnp.bfloat16
HIGH = lax.Precision.HIGHEST
GROUP = 16


def dot_nt(a, b):
    return lax.dot_general(a, b, (((1,), (1,)), ((), ())), preferred_element_type=F32)


def dot_high(a, b):
    return lax.dot_general(
        a, b, (((1,), (0,)), ((), ())), precision=HIGH, preferred_element_type=F32
    )


def kernel(
    n_key,
    n_head,
    q_h,
    k_h,
    v_h,
    dg_h,
    wg_h,
    ridge_ref,
    gain_h,
    cov_h,
    vs_h,
    w_h,
    out_ref,
    q_v,
    k_v,
    v_v,
    dg_v,
    wg_v,
    gain_v,
    cov_v,
    vs_v,
    w_v,
    dgx,
    wgx,
    kf,
    vf,
    dref,
    rref,
    xref,
    bref,
    img,
    rd_send,
    rd_recv,
    den_send,
    den_recv,
    sq_send,
    sq_recv,
    core_send,
    core_recv,
    own,
    x_send,
    x_recv,
    keep,
    z_send,
    z_recv,
    in_sem,
    cov_sem,
    vs_sem,
    w_sem,
    img_ss,
    img_rs,
    rd_ss,
    rd_rs,
    den_ss,
    den_rs,
    sq_ss,
    sq_rs,
    core_ss,
    core_rs,
    x_ss,
    x_rs,
    z_ss,
    z_rs,
):
    key = lax.axis_index("key")
    head = lax.axis_index("head")
    seqs, draft, width = q_v.shape
    rows = cov_v.shape[1]
    values = vs_v.shape[1]
    vcols = values // n_key
    n = seqs * draft
    block = out_ref.shape[1]
    per_group = GROUP // draft

    barrier = pltpu.get_barrier_semaphore()
    for d in range(1, n_key):
        pl.semaphore_signal(
            barrier, inc=1, device_id={"key": lax.rem(key + d, n_key)}, device_id_type=MESH
        )
    for d in range(1, n_head):
        pl.semaphore_signal(
            barrier, inc=1, device_id={"head": lax.rem(head + d, n_head)}, device_id_type=MESH
        )

    small = []
    pairs = ((q_h.at[:, 0], q_v), (k_h.at[:, 0], k_v), (dg_h, dg_v), (wg_h, wg_v), (v_h.at[:, 0], v_v), (gain_h, gain_v))
    for i, (src, dst) in enumerate(pairs):
        small.append(pltpu.make_async_copy(src, dst, in_sem.at[i]))
    cov_in = [pltpu.make_async_copy(cov_h.at[s, 0], cov_v.at[s], cov_sem.at[s]) for s in range(seqs)]
    vs_in = [pltpu.make_async_copy(vs_h.at[s, 0], vs_v.at[s], vs_sem.at[s]) for s in range(seqs)]
    w_in = pltpu.make_async_copy(w_h.at[0], w_v, w_sem)
    for c in small + cov_in + vs_in + [w_in]:
        c.start()
    for c in small:
        c.wait()

    for s in range(seqs):
        at = pl.ds(s * draft, draft)
        dref[at, :] = q_v[s].astype(F32)
        kf[at, :] = k_v[s].astype(F32)
        vf[at, :] = v_v[s].astype(F32)
        dgx[at, :] = jnp.broadcast_to(dg_v[s], (draft, draft))
        wgx[at, :] = jnp.broadcast_to(wg_v[s], (draft, draft))

    row_id = lax.broadcasted_iota(jnp.int32, (n, 1), 0)
    tok = lax.rem(row_id, draft)
    first = row_id - tok
    gates, writes = dgx[...], wgx[...]
    totals = [gates[:, 0:1]]
    for u in range(1, draft):
        totals.append(totals[-1] * gates[:, u : u + 1])
    decay = totals[0]
    for u in range(1, draft):
        decay = jnp.where(tok == u, totals[u], decay)
    col_id = lax.broadcasted_iota(jnp.int32, (n, n), 1)
    mix = jnp.zeros((n, n), F32)
    for u in range(draft):
        weight = writes[:, u : u + 1] * (decay / totals[u])
        mix = jnp.where((col_id == first + u) & (tok >= u), weight, mix)
    lane = lax.broadcasted_iota(jnp.int32, (n, 128), 1)
    diag = lane == lax.broadcasted_iota(jnp.int32, (n, 128), 0)

    def as_row(column):
        row = jnp.sum(jnp.where(diag, column, 0.0), axis=0, keepdims=True)
        return jnp.broadcast_to(row, (8, 128))

    def as_column(row):
        return jnp.sum(jnp.where(diag, row[0:1, :], 0.0), axis=1, keepdims=True)

    ridge = ridge_ref[0]
    keys = kf[...]
    keys_b = keys.astype(BF16)
    group_row = lax.broadcasted_iota(jnp.int32, (GROUP, 1), 0) // draft

    def local_product(dir_b, wait):
        parts = []
        for g in range(n // GROUP):
            lhs = dir_b[g * GROUP : (g + 1) * GROUP]
            acc = None
            for j in range(per_group):
                s = g * per_group + j
                if wait:
                    cov_in[s].wait()
                prod = dot_nt(lhs, cov_v[s])
                acc = prod if acc is None else jnp.where(group_row == j, prod, acc)
            parts.append(acc)
        return decay * jnp.concatenate(parts, axis=0)

    mine = pl.ds(pl.multiple_of(key * rows, 128), rows)
    direction = dref[...]
    rref[...] = direction
    sq_norm = jnp.sum(direction * direction, axis=1, keepdims=True)
    sends = []
    for it in range(ITERS - 1):
        dir_b = dref[...].astype(BF16)
        img[it, key] = local_product(dir_b, it == 0)
        if it == 0:
            pl.semaphore_wait(barrier, n_key - 1 + n_head - 1)
        copies = []
        for d in range(1, n_key):
            c = pltpu.make_async_remote_copy(
                src_ref=img.at[it, key],
                dst_ref=img.at[it, key],
                send_sem=img_ss.at[it, d],
                recv_sem=img_rs.at[it, d],
                device_id={"key": lax.rem(key + d, n_key)},
                device_id_type=MESH,
            )
            c.start()
            copies.append(c)
        dots = dot_nt(dir_b, keys_b)
        bref[...] = dot_high(mix * dots, keys) + ridge * dref[...]
        for c in copies:
            c.wait_recv()
        sends += copies
        applied = jnp.concatenate([img[it, j] for j in range(n_key)], axis=1) + bref[...]
        direction = dref[...]
        step = sq_norm / jnp.sum(direction * applied, axis=1, keepdims=True)
        if it == 0:
            xref[...] = step * direction
        else:
            xref[...] = xref[...] + step * direction
        residual = rref[...] - step * applied
        rref[...] = residual
        new_norm = jnp.sum(residual * residual, axis=1, keepdims=True)
        dref[...] = residual + (new_norm / sq_norm) * direction
        sq_norm = new_norm

    dir_b = dref[...].astype(BF16)
    image = local_product(dir_b, False)
    den_send[...] = as_row(jnp.sum(image * dref[:, mine], axis=1, keepdims=True))
    for d in range(1, n_key):
        c = pltpu.make_async_remote_copy(
            src_ref=den_send,
            dst_ref=den_recv.at[d],
            send_sem=den_ss.at[d],
            recv_sem=den_rs.at[d],
            device_id={"key": lax.rem(key + d, n_key)},
            device_id_type=MESH,
        )
        c.start()
        sends.append(c)
    dens = sends[-(n_key - 1) :]

    x_rows = xref[:, mine].astype(BF16)
    d_rows = dref[:, mine].astype(BF16)
    for g in range(n // GROUP):
        at = slice(g * GROUP, (g + 1) * GROUP)
        lhs = jnp.concatenate([x_rows[at], d_rows[at]], axis=0)
        acc_x = acc_d = None
        for j in range(per_group):
            s = g * per_group + j
            vs_in[s].wait()
            prod = dot_nt(lhs, vs_v[s])
            px, pd = prod[:GROUP], prod[GROUP:]
            acc_x = px if acc_x is None else jnp.where(group_row == j, px, acc_x)
            acc_d = pd if acc_d is None else jnp.where(group_row == j, pd, acc_d)
        acc_x = (decay[at] * acc_x).astype(BF16)
        acc_d = (decay[at] * acc_d).astype(BF16)
        for j in range(n_key):
            cols = slice(j * vcols, (j + 1) * vcols)
            rd_send[j, 0, at, :] = acc_x[:, cols]
            rd_send[j, 1, at, :] = acc_d[:, cols]
    reads = []
    for d in range(1, n_key):
        to = lax.rem(key + d, n_key)
        c = pltpu.make_async_remote_copy(
            src_ref=rd_send.at[to],
            dst_ref=rd_recv.at[d],
            send_sem=rd_ss.at[d],
            recv_sem=rd_rs.at[d],
            device_id={"key": to},
            device_id_type=MESH,
        )
        c.start()
        reads.append(c)
    sends += reads
    dots_d = dot_nt(dir_b, keys_b)
    dots_x = dot_nt(xref[...].astype(BF16), keys_b)
    base = dot_high(mix * dots_d, keys) + ridge * dref[...]
    den = jnp.sum(base * dref[...], axis=1, keepdims=True) + as_column(den_send[...])
    vcol = pl.ds(pl.multiple_of(key * vcols, 128), vcols)
    vals = vf[:, vcol]
    read_x = dot_high(mix * dots_x, vals) + rd_send[key, 0].astype(F32)
    read_d = dot_high(mix * dots_d, vals) + rd_send[key, 1].astype(F32)
    for d in range(1, n_key):
        dens[d - 1].wait_recv()
        den = den + as_column(den_recv[d])
    step = sq_norm / den
    for d in range(1, n_key):
        reads[d - 1].wait_recv()
        read_x = read_x + rd_recv[d, 0].astype(F32)
        read_d = read_d + rd_recv[d, 1].astype(F32)
    read = read_x + step * read_d

    sq_send[...] = as_row(jnp.sum(read * read, axis=1, keepdims=True))
    squares = []
    for d in range(1, n_key):
        c = pltpu.make_async_remote_copy(
            src_ref=sq_send,
            dst_ref=sq_recv.at[d],
            send_sem=sq_ss.at[d],
            recv_sem=sq_rs.at[d],
            device_id={"key": lax.rem(key + d, n_key)},
            device_id_type=MESH,
        )
        c.start()
        squares.append(c)
    sends += squares
    gained = (read * gain_v[...]).astype(BF16)
    w_in.wait()

    core = lax.rem(key, 2)
    chip = key // 2
    partner = key + 1 - 2 * core
    across = lax.rem(key + 2, n_key)

    def project(to_key, to_head):
        at = pl.multiple_of((to_key * n_head + to_head) * block, 128)
        return jnp.dot(gained, w_v[:, pl.ds(at, block)], preferred_element_type=F32)

    order = list(range(1, n_head)) + [0]
    core_copy, x_copy, z_copy = {}, {}, {}
    scale = []

    def stage_a(o):
        to = lax.rem(head + o, n_head)
        for half in range(2):
            core_send[o, half] = project(2 * half + 1 - core, to).astype(BF16)
        c = pltpu.make_async_remote_copy(
            src_ref=core_send.at[o],
            dst_ref=core_recv.at[o],
            send_sem=core_ss.at[o],
            recv_sem=core_rs.at[o],
            device_id={"key": partner},
            device_id_type=MESH,
        )
        c.start()
        core_copy[o] = c
        for half in range(2):
            own[o, half] = project(2 * half + core, to)

    def stage_b(o):
        core_copy[o].wait_recv()
        other = 1 - chip
        x_send[o] = (own[o, other] + core_recv[o, other].astype(F32)).astype(BF16)
        c = pltpu.make_async_remote_copy(
            src_ref=x_send.at[o],
            dst_ref=x_recv.at[o],
            send_sem=x_ss.at[o],
            recv_sem=x_rs.at[o],
            device_id={"key": across},
            device_id_type=MESH,
        )
        c.start()
        x_copy[o] = c
        keep[o] = own[o, chip] + core_recv[o, chip].astype(F32)

    def stage_c(o):
        if not scale:
            total = as_column(sq_send[...])
            for d in range(1, n_key):
                squares[d - 1].wait_recv()
                total = total + as_column(sq_recv[d])
            scale.append(lax.rsqrt(total / values + 1e-06))
        x_copy[o].wait_recv()
        done = (keep[o] + x_recv[o].astype(F32)) * scale[0]
        if o == 0:
            keep[o] = done
            return
        z_send[o] = done.astype(BF16)
        c = pltpu.make_async_remote_copy(
            src_ref=z_send.at[o],
            dst_ref=z_recv.at[o],
            send_sem=z_ss.at[o],
            recv_sem=z_rs.at[o],
            device_id={"head": lax.rem(head + o, n_head)},
            device_id_type=MESH,
        )
        c.start()
        z_copy[o] = c

    for i in range(n_head + 2):
        if i < n_head:
            stage_a(order[i])
        if 0 <= i - 1 < n_head:
            stage_b(order[i - 1])
        if 0 <= i - 2 < n_head:
            stage_c(order[i - 2])
    result = keep[0]
    for o in range(1, n_head):
        z_copy[o].wait_recv()
        result = result + z_recv[o].astype(F32)
    out_ref[...] = result
    for c in sends + list(core_copy.values()) + list(x_copy.values()) + list(z_copy.values()):
        c.wait_send()


def solution(mesh):
    n_key, n_head = mesh.shape["key"], mesh.shape["head"]
    assert n_key == 4

    def body(q, k, v, dg, wg, ridge, gain, cov, vs, w):
        seqs, _, draft, width = q.shape
        rows = cov.shape[2]
        values = vs.shape[2]
        vcols = values // n_key
        model = w.shape[2]
        block = model // (n_key * n_head)
        n = seqs * draft
        dma = pltpu.SemaphoreType.DMA
        out = pl.pallas_call(
            functools.partial(kernel, n_key, n_head),
            out_shape=jax.ShapeDtypeStruct((n, block), F32),
            in_specs=[pl.BlockSpec(memory_space=pl.ANY)] * 5
            + [pl.BlockSpec(memory_space=pltpu.SMEM)]
            + [pl.BlockSpec(memory_space=pl.ANY)] * 4,
            out_specs=pl.BlockSpec(memory_space=pltpu.VMEM),
            scratch_shapes=[
                pltpu.VMEM((seqs, draft, width), BF16),
                pltpu.VMEM((seqs, draft, width), BF16),
                pltpu.VMEM((seqs, draft, values), BF16),
                pltpu.VMEM(dg.shape, F32),
                pltpu.VMEM(wg.shape, F32),
                pltpu.VMEM(gain.shape, F32),
                pltpu.VMEM((seqs, rows, width), BF16),
                pltpu.VMEM((seqs, values, rows), BF16),
                pltpu.VMEM(w.shape[1:], BF16),
                pltpu.VMEM((n, draft), F32),
                pltpu.VMEM((n, draft), F32),
                pltpu.VMEM((n, width), F32),
                pltpu.VMEM((n, values), F32),
                pltpu.VMEM((n, width), F32),
                pltpu.VMEM((n, width), F32),
                pltpu.VMEM((n, width), F32),
                pltpu.VMEM((n, width), F32),
                pltpu.VMEM((ITERS - 1, n_key, n, rows), F32),
                pltpu.VMEM((n_key, 2, n, vcols), BF16),
                pltpu.VMEM((n_key, 2, n, vcols), BF16),
                pltpu.VMEM((8, 128), F32),
                pltpu.VMEM((n_key, 8, 128), F32),
                pltpu.VMEM((8, 128), F32),
                pltpu.VMEM((n_key, 8, 128), F32),
                pltpu.VMEM((n_head, 2, n, block), BF16),
                pltpu.VMEM((n_head, 2, n, block), BF16),
                pltpu.VMEM((n_head, 2, n, block), F32),
                pltpu.VMEM((n_head, n, block), BF16),
                pltpu.VMEM((n_head, n, block), BF16),
                pltpu.VMEM((n_head, n, block), F32),
                pltpu.VMEM((n_head, n, block), BF16),
                pltpu.VMEM((n_head, n, block), BF16),
                dma((6,)),
                dma((seqs,)),
                dma((seqs,)),
                dma,
                dma((ITERS - 1, n_key)),
                dma((ITERS - 1, n_key)),
                dma((n_key,)),
                dma((n_key,)),
                dma((n_key,)),
                dma((n_key,)),
                dma((n_key,)),
                dma((n_key,)),
                dma((n_head,)),
                dma((n_head,)),
                dma((n_head,)),
                dma((n_head,)),
                dma((n_head,)),
                dma((n_head,)),
            ],
            compiler_params=pltpu.CompilerParams(collective_id=0, has_side_effects=True),
        )(q, k, v, dg, wg, ridge, gain, cov, vs, w)
        return out.astype(BF16).reshape(seqs, draft, block)

    placed = (
        P("batch", "head", None, None),
        P("batch", "head", None, None),
        P("batch", "head", None, None),
        P("batch", "head", None),
        P("batch", "head", None),
        P("head"),
        P("head", "key"),
        P("batch", "head", "key", None),
        P("batch", "head", None, "key"),
        P("head", "key", None),
    )
    return jax.shard_map(
        body,
        mesh=mesh,
        in_specs=placed,
        out_specs=P("batch", None, ("key", "head")),
        check_vma=False,
    )
```

```python
import functools

import jax
import jax.numpy as jnp
from jax import lax
from jax.experimental import pallas as pl
from jax.experimental.pallas import tpu as pltpu
from jax.sharding import PartitionSpec as P

ITERS = 3
MESH = pl.DeviceIdType.MESH
F32 = jnp.float32
BF16 = jnp.bfloat16
HIGH = lax.Precision.HIGHEST
GROUP = 16


def dot_nt(a, b):
    return lax.dot_general(a, b, (((1,), (1,)), ((), ())), preferred_element_type=F32)


def dot_high(a, b):
    return lax.dot_general(
        a, b, (((1,), (0,)), ((), ())), precision=HIGH, preferred_element_type=F32
    )


def kernel(
    n_key,
    n_head,
    q_h,
    k_h,
    v_h,
    dg_h,
    wg_h,
    ridge_ref,
    gain_h,
    cov_h,
    vs_h,
    w_h,
    out_ref,
    q_v,
    k_v,
    v_v,
    dg_v,
    wg_v,
    gain_v,
    cov_v,
    vs_v,
    w_v,
    kf,
    vf,
    dref,
    rref,
    xref,
    bref,
    img,
    rd_send,
    rd_recv,
    den_send,
    den_recv,
    sq_send,
    sq_recv,
    core_send,
    core_recv,
    own,
    x_send,
    x_recv,
    keep,
    z_send,
    z_recv,
    in_sem,
    cov_sem,
    vs_sem,
    w_sem,
    img_ss,
    img_rs,
    rd_ss,
    rd_rs,
    den_ss,
    den_rs,
    sq_ss,
    sq_rs,
    core_ss,
    core_rs,
    x_ss,
    x_rs,
    z_ss,
    z_rs,
):
    key = lax.axis_index("key")
    head = lax.axis_index("head")
    seqs, draft, width = q_v.shape
    rows = cov_v.shape[1]
    values = vs_v.shape[1]
    vcols = values // n_key
    n = seqs * draft
    block = out_ref.shape[2]
    per_group = GROUP // draft

    barrier = pltpu.get_barrier_semaphore()
    for d in range(1, n_key):
        pl.semaphore_signal(
            barrier, inc=1, device_id={"key": lax.rem(key + d, n_key)}, device_id_type=MESH
        )
    for d in range(1, n_head):
        pl.semaphore_signal(
            barrier, inc=1, device_id={"head": lax.rem(head + d, n_head)}, device_id_type=MESH
        )

    small = []
    pairs = ((q_h.at[:, 0], q_v), (k_h.at[:, 0], k_v), (dg_h, dg_v), (wg_h, wg_v), (v_h.at[:, 0], v_v), (gain_h, gain_v))
    for i, (src, dst) in enumerate(pairs):
        small.append(pltpu.make_async_copy(src, dst, in_sem.at[i]))
    cov_in = [pltpu.make_async_copy(cov_h.at[s, 0], cov_v.at[s], cov_sem.at[s]) for s in range(seqs)]
    vs_in = [pltpu.make_async_copy(vs_h.at[s, 0], vs_v.at[s], vs_sem.at[s]) for s in range(seqs)]
    w_in = pltpu.make_async_copy(w_h.at[0], w_v, w_sem)
    for c in small + cov_in + vs_in + [w_in]:
        c.start()
    for c in small:
        c.wait()

    for s in range(seqs):
        at = pl.ds(s * draft, draft)
        dref[at, :] = q_v[s].astype(F32)
        kf[at, :] = k_v[s].astype(F32)
        vf[at, :] = v_v[s].astype(F32)

    row_id = lax.broadcasted_iota(jnp.int32, (n, 1), 0)
    tok = lax.rem(row_id, draft)
    first = row_id - tok
    seq_hot = lax.broadcasted_iota(jnp.int32, (n, seqs), 1) == row_id // draft

    def per_row(gates, u):
        return jnp.sum(jnp.where(seq_hot, gates[u : u + 1, :], 0.0), axis=1, keepdims=True)

    gates, writes = dg_v[0], wg_v[0]
    totals = [per_row(gates, 0)]
    for u in range(1, draft):
        totals.append(totals[-1] * per_row(gates, u))
    decay = totals[0]
    for u in range(1, draft):
        decay = jnp.where(tok == u, totals[u], decay)
    col_id = lax.broadcasted_iota(jnp.int32, (n, n), 1)
    mix = jnp.zeros((n, n), F32)
    for u in range(draft):
        weight = per_row(writes, u) * (decay / totals[u])
        mix = jnp.where((col_id == first + u) & (tok >= u), weight, mix)
    lane = lax.broadcasted_iota(jnp.int32, (n, 128), 1)
    diag = lane == lax.broadcasted_iota(jnp.int32, (n, 128), 0)

    def as_row(column):
        row = jnp.sum(jnp.where(diag, column, 0.0), axis=0, keepdims=True)
        return jnp.broadcast_to(row, (8, 128))

    def as_column(row):
        return jnp.sum(jnp.where(diag, row[0:1, :], 0.0), axis=1, keepdims=True)

    ridge = ridge_ref[0]
    keys = kf[...]
    keys_b = keys.astype(BF16)
    group_row = lax.broadcasted_iota(jnp.int32, (GROUP, 1), 0) // draft

    def local_product(dir_b, wait):
        parts = []
        for g in range(n // GROUP):
            lhs = dir_b[g * GROUP : (g + 1) * GROUP]
            acc = None
            for j in range(per_group):
                s = g * per_group + j
                if wait:
                    cov_in[s].wait()
                prod = dot_nt(lhs, cov_v[s])
                acc = prod if acc is None else jnp.where(group_row == j, prod, acc)
            parts.append(acc)
        return decay * jnp.concatenate(parts, axis=0)

    mine = pl.ds(pl.multiple_of(key * rows, 128), rows)
    direction = dref[...]
    rref[...] = direction
    sq_norm = jnp.sum(direction * direction, axis=1, keepdims=True)
    sends = []
    for it in range(ITERS - 1):
        dir_b = dref[...].astype(BF16)
        img[it, key] = local_product(dir_b, it == 0)
        if it == 0:
            pl.semaphore_wait(barrier, n_key - 1 + n_head - 1)
        copies = []
        for d in range(1, n_key):
            c = pltpu.make_async_remote_copy(
                src_ref=img.at[it, key],
                dst_ref=img.at[it, key],
                send_sem=img_ss.at[it, d],
                recv_sem=img_rs.at[it, d],
                device_id={"key": lax.rem(key + d, n_key)},
                device_id_type=MESH,
            )
            c.start()
            copies.append(c)
        dots = dot_nt(dir_b, keys_b)
        bref[...] = dot_high(mix * dots, keys) + ridge * dref[...]
        for c in copies:
            c.wait_recv()
        sends += copies
        applied = jnp.concatenate([img[it, j] for j in range(n_key)], axis=1) + bref[...]
        direction = dref[...]
        step = sq_norm / jnp.sum(direction * applied, axis=1, keepdims=True)
        if it == 0:
            xref[...] = step * direction
        else:
            xref[...] = xref[...] + step * direction
        residual = rref[...] - step * applied
        rref[...] = residual
        new_norm = jnp.sum(residual * residual, axis=1, keepdims=True)
        dref[...] = residual + (new_norm / sq_norm) * direction
        sq_norm = new_norm

    dir_b = dref[...].astype(BF16)
    image = local_product(dir_b, False)
    den_send[...] = as_row(jnp.sum(image * dref[:, mine], axis=1, keepdims=True))
    for d in range(1, n_key):
        c = pltpu.make_async_remote_copy(
            src_ref=den_send,
            dst_ref=den_recv.at[d],
            send_sem=den_ss.at[d],
            recv_sem=den_rs.at[d],
            device_id={"key": lax.rem(key + d, n_key)},
            device_id_type=MESH,
        )
        c.start()
        sends.append(c)
    dens = sends[-(n_key - 1) :]

    x_rows = xref[:, mine].astype(BF16)
    d_rows = dref[:, mine].astype(BF16)
    for g in range(n // GROUP):
        at = slice(g * GROUP, (g + 1) * GROUP)
        lhs = jnp.concatenate([x_rows[at], d_rows[at]], axis=0)
        acc_x = acc_d = None
        for j in range(per_group):
            s = g * per_group + j
            vs_in[s].wait()
            prod = dot_nt(lhs, vs_v[s])
            px, pd = prod[:GROUP], prod[GROUP:]
            acc_x = px if acc_x is None else jnp.where(group_row == j, px, acc_x)
            acc_d = pd if acc_d is None else jnp.where(group_row == j, pd, acc_d)
        acc_x = (decay[at] * acc_x).astype(BF16)
        acc_d = (decay[at] * acc_d).astype(BF16)
        for j in range(n_key):
            cols = slice(j * vcols, (j + 1) * vcols)
            rd_send[j, 0, at, :] = acc_x[:, cols]
            rd_send[j, 1, at, :] = acc_d[:, cols]
    reads = []
    for d in range(1, n_key):
        to = lax.rem(key + d, n_key)
        c = pltpu.make_async_remote_copy(
            src_ref=rd_send.at[to],
            dst_ref=rd_recv.at[d],
            send_sem=rd_ss.at[d],
            recv_sem=rd_rs.at[d],
            device_id={"key": to},
            device_id_type=MESH,
        )
        c.start()
        reads.append(c)
    sends += reads
    dots_d = dot_nt(dir_b, keys_b)
    dots_x = dot_nt(xref[...].astype(BF16), keys_b)
    base = dot_high(mix * dots_d, keys) + ridge * dref[...]
    den = jnp.sum(base * dref[...], axis=1, keepdims=True) + as_column(den_send[...])
    vcol = pl.ds(pl.multiple_of(key * vcols, 128), vcols)
    vals = vf[:, vcol]
    read_x = dot_high(mix * dots_x, vals) + rd_send[key, 0].astype(F32)
    read_d = dot_high(mix * dots_d, vals) + rd_send[key, 1].astype(F32)
    for d in range(1, n_key):
        dens[d - 1].wait_recv()
        den = den + as_column(den_recv[d])
    step = sq_norm / den
    for d in range(1, n_key):
        reads[d - 1].wait_recv()
        read_x = read_x + rd_recv[d, 0].astype(F32)
        read_d = read_d + rd_recv[d, 1].astype(F32)
    read = read_x + step * read_d

    sq_send[...] = as_row(jnp.sum(read * read, axis=1, keepdims=True))
    squares = []
    for d in range(1, n_key):
        c = pltpu.make_async_remote_copy(
            src_ref=sq_send,
            dst_ref=sq_recv.at[d],
            send_sem=sq_ss.at[d],
            recv_sem=sq_rs.at[d],
            device_id={"key": lax.rem(key + d, n_key)},
            device_id_type=MESH,
        )
        c.start()
        squares.append(c)
    sends += squares
    gained = (read * gain_v[...]).astype(BF16)
    w_in.wait()

    core = lax.rem(key, 2)
    chip = key // 2
    partner = key + 1 - 2 * core
    across = lax.rem(key + 2, n_key)

    def project(to_key, to_head):
        at = pl.multiple_of((to_key * n_head + to_head) * block, 128)
        return jnp.dot(gained, w_v[:, pl.ds(at, block)], preferred_element_type=F32)

    order = list(range(1, n_head)) + [0]
    core_copy, x_copy, z_copy = {}, {}, {}
    scale = []

    def stage_a(o):
        to = lax.rem(head + o, n_head)
        for half in range(2):
            core_send[o, half] = project(2 * half + 1 - core, to).astype(BF16)
        c = pltpu.make_async_remote_copy(
            src_ref=core_send.at[o],
            dst_ref=core_recv.at[o],
            send_sem=core_ss.at[o],
            recv_sem=core_rs.at[o],
            device_id={"key": partner},
            device_id_type=MESH,
        )
        c.start()
        core_copy[o] = c
        for half in range(2):
            own[o, half] = project(2 * half + core, to)

    def stage_b(o):
        core_copy[o].wait_recv()
        other = 1 - chip
        x_send[o] = (own[o, other] + core_recv[o, other].astype(F32)).astype(BF16)
        c = pltpu.make_async_remote_copy(
            src_ref=x_send.at[o],
            dst_ref=x_recv.at[o],
            send_sem=x_ss.at[o],
            recv_sem=x_rs.at[o],
            device_id={"key": across},
            device_id_type=MESH,
        )
        c.start()
        x_copy[o] = c
        keep[o] = own[o, chip] + core_recv[o, chip].astype(F32)

    def stage_c(o):
        if not scale:
            total = as_column(sq_send[...])
            for d in range(1, n_key):
                squares[d - 1].wait_recv()
                total = total + as_column(sq_recv[d])
            scale.append(lax.rsqrt(total / values + 1e-06))
        x_copy[o].wait_recv()
        done = (keep[o] + x_recv[o].astype(F32)) * scale[0]
        if o == 0:
            keep[o] = done
            return
        z_send[o] = done.astype(BF16)
        c = pltpu.make_async_remote_copy(
            src_ref=z_send.at[o],
            dst_ref=z_recv.at[o],
            send_sem=z_ss.at[o],
            recv_sem=z_rs.at[o],
            device_id={"head": lax.rem(head + o, n_head)},
            device_id_type=MESH,
        )
        c.start()
        z_copy[o] = c

    for i in range(n_head + 2):
        if i < n_head:
            stage_a(order[i])
        if 0 <= i - 1 < n_head:
            stage_b(order[i - 1])
        if 0 <= i - 2 < n_head:
            stage_c(order[i - 2])
    result = keep[0]
    for o in range(1, n_head):
        z_copy[o].wait_recv()
        result = result + z_recv[o].astype(F32)
    keep[0] = result
    for s in range(seqs):
        out_ref[s] = keep[0, s * draft : (s + 1) * draft, :].astype(BF16)
    for c in sends + list(core_copy.values()) + list(x_copy.values()) + list(z_copy.values()):
        c.wait_send()


def solution(mesh):
    n_key, n_head = mesh.shape["key"], mesh.shape["head"]
    assert n_key == 4

    def body(q, k, v, dg, wg, ridge, gain, cov, vs, w):
        seqs, _, draft, width = q.shape
        rows = cov.shape[2]
        values = vs.shape[2]
        vcols = values // n_key
        model = w.shape[2]
        block = model // (n_key * n_head)
        n = seqs * draft
        dma = pltpu.SemaphoreType.DMA
        out = pl.pallas_call(
            functools.partial(kernel, n_key, n_head),
            out_shape=jax.ShapeDtypeStruct((seqs, draft, block), BF16),
            in_specs=[pl.BlockSpec(memory_space=pl.ANY)] * 5
            + [pl.BlockSpec(memory_space=pltpu.SMEM)]
            + [pl.BlockSpec(memory_space=pl.ANY)] * 4,
            out_specs=pl.BlockSpec(memory_space=pltpu.VMEM),
            scratch_shapes=[
                pltpu.VMEM((seqs, draft, width), BF16),
                pltpu.VMEM((seqs, draft, width), BF16),
                pltpu.VMEM((seqs, draft, values), BF16),
                pltpu.VMEM((1, draft, seqs), F32),
                pltpu.VMEM((1, draft, seqs), F32),
                pltpu.VMEM(gain.shape, F32),
                pltpu.VMEM((seqs, rows, width), BF16),
                pltpu.VMEM((seqs, values, rows), BF16),
                pltpu.VMEM(w.shape[1:], BF16),
                pltpu.VMEM((n, width), F32),
                pltpu.VMEM((n, values), F32),
                pltpu.VMEM((n, width), F32),
                pltpu.VMEM((n, width), F32),
                pltpu.VMEM((n, width), F32),
                pltpu.VMEM((n, width), F32),
                pltpu.VMEM((ITERS - 1, n_key, n, rows), F32),
                pltpu.VMEM((n_key, 2, n, vcols), BF16),
                pltpu.VMEM((n_key, 2, n, vcols), BF16),
                pltpu.VMEM((8, 128), F32),
                pltpu.VMEM((n_key, 8, 128), F32),
                pltpu.VMEM((8, 128), F32),
                pltpu.VMEM((n_key, 8, 128), F32),
                pltpu.VMEM((n_head, 2, n, block), BF16),
                pltpu.VMEM((n_head, 2, n, block), BF16),
                pltpu.VMEM((n_head, 2, n, block), F32),
                pltpu.VMEM((n_head, n, block), BF16),
                pltpu.VMEM((n_head, n, block), BF16),
                pltpu.VMEM((n_head, n, block), F32),
                pltpu.VMEM((n_head, n, block), BF16),
                pltpu.VMEM((n_head, n, block), BF16),
                dma((6,)),
                dma((seqs,)),
                dma((seqs,)),
                dma,
                dma((ITERS - 1, n_key)),
                dma((ITERS - 1, n_key)),
                dma((n_key,)),
                dma((n_key,)),
                dma((n_key,)),
                dma((n_key,)),
                dma((n_key,)),
                dma((n_key,)),
                dma((n_head,)),
                dma((n_head,)),
                dma((n_head,)),
                dma((n_head,)),
                dma((n_head,)),
                dma((n_head,)),
            ],
            compiler_params=pltpu.CompilerParams(collective_id=0, has_side_effects=True),
        )(
            q,
            k,
            v,
            dg.transpose(1, 2, 0),
            wg.transpose(1, 2, 0),
            ridge,
            gain,
            cov,
            vs,
            w,
        )
        return out

    placed = (
        P("batch", "head", None, None),
        P("batch", "head", None, None),
        P("batch", "head", None, None),
        P("batch", "head", None),
        P("batch", "head", None),
        P("head"),
        P("head", "key"),
        P("batch", "head", "key", None),
        P("batch", "head", None, "key"),
        P("head", "key", None),
    )
    return jax.shard_map(
        body,
        mesh=mesh,
        in_specs=placed,
        out_specs=P("batch", None, ("key", "head")),
        check_vma=False,
    )
```

```python
import functools

import jax
import jax.numpy as jnp
from jax import lax
from jax.experimental import pallas as pl
from jax.experimental.pallas import tpu as pltpu
from jax.sharding import PartitionSpec as P

ITERS = 3
MESH = pl.DeviceIdType.MESH
F32 = jnp.float32
BF16 = jnp.bfloat16
HIGH = lax.Precision.HIGHEST
GROUP = 16


def dot_nt(a, b):
    return lax.dot_general(a, b, (((1,), (1,)), ((), ())), preferred_element_type=F32)


def dot_high(a, b):
    return lax.dot_general(
        a, b, (((1,), (0,)), ((), ())), precision=HIGH, preferred_element_type=F32
    )


def kernel(
    n_key,
    n_head,
    q_h,
    k_h,
    v_h,
    dg_h,
    wg_h,
    ridge_ref,
    gain_h,
    cov_h,
    vs_h,
    w_h,
    out_ref,
    q_v,
    k_v,
    v_v,
    dg_v,
    wg_v,
    gain_v,
    cov_v,
    vs_v,
    w_v,
    kf,
    vf,
    dref,
    rref,
    xref,
    bref,
    img,
    rd_send,
    rd_recv,
    den_send,
    den_recv,
    sq_send,
    sq_recv,
    core_send,
    core_recv,
    own,
    x_send,
    x_recv,
    keep,
    z_send,
    z_recv,
    in_sem,
    cov_sem,
    vs_sem,
    w_sem,
    img_ss,
    img_rs,
    rd_ss,
    rd_rs,
    den_ss,
    den_rs,
    sq_ss,
    sq_rs,
    core_ss,
    core_rs,
    x_ss,
    x_rs,
    z_ss,
    z_rs,
):
    key = lax.axis_index("key")
    head = lax.axis_index("head")
    seqs, draft, width = q_v.shape
    rows = cov_v.shape[1]
    values = vs_v.shape[1]
    vcols = values // n_key
    n = seqs * draft
    block = out_ref.shape[2]
    per_group = GROUP // draft

    barrier = pltpu.get_barrier_semaphore()
    for d in range(1, n_key):
        pl.semaphore_signal(
            barrier, inc=1, device_id={"key": lax.rem(key + d, n_key)}, device_id_type=MESH
        )
    for d in range(1, n_head):
        pl.semaphore_signal(
            barrier, inc=1, device_id={"head": lax.rem(head + d, n_head)}, device_id_type=MESH
        )

    small = []
    pairs = ((q_h.at[:, 0], q_v), (k_h.at[:, 0], k_v), (dg_h, dg_v), (wg_h, wg_v), (v_h.at[:, 0], v_v), (gain_h, gain_v))
    for i, (src, dst) in enumerate(pairs):
        small.append(pltpu.make_async_copy(src, dst, in_sem.at[i]))
    cov_in = [pltpu.make_async_copy(cov_h.at[s, 0], cov_v.at[s], cov_sem.at[s]) for s in range(seqs)]
    vs_in = [pltpu.make_async_copy(vs_h.at[s, 0], vs_v.at[s], vs_sem.at[s]) for s in range(seqs)]
    w_in = pltpu.make_async_copy(w_h.at[0], w_v, w_sem)
    for c in small + cov_in:
        c.start()
    for c in small:
        c.wait()

    for s in range(seqs):
        at = pl.ds(s * draft, draft)
        dref[at, :] = q_v[s].astype(F32)
        kf[at, :] = k_v[s].astype(F32)
        vf[at, :] = v_v[s].astype(F32)

    row_id = lax.broadcasted_iota(jnp.int32, (n, 1), 0)
    tok = lax.rem(row_id, draft)
    first = row_id - tok
    seq_hot = lax.broadcasted_iota(jnp.int32, (n, seqs), 1) == row_id // draft

    def per_row(gates, u):
        return jnp.sum(jnp.where(seq_hot, gates[u : u + 1, :], 0.0), axis=1, keepdims=True)

    gates, writes = dg_v[0], wg_v[0]
    totals = [per_row(gates, 0)]
    for u in range(1, draft):
        totals.append(totals[-1] * per_row(gates, u))
    decay = totals[0]
    for u in range(1, draft):
        decay = jnp.where(tok == u, totals[u], decay)
    col_id = lax.broadcasted_iota(jnp.int32, (n, n), 1)
    mix = jnp.zeros((n, n), F32)
    for u in range(draft):
        weight = per_row(writes, u) * (decay / totals[u])
        mix = jnp.where((col_id == first + u) & (tok >= u), weight, mix)
    lane = lax.broadcasted_iota(jnp.int32, (n, 128), 1)
    diag = lane == lax.broadcasted_iota(jnp.int32, (n, 128), 0)

    def as_row(column):
        row = jnp.sum(jnp.where(diag, column, 0.0), axis=0, keepdims=True)
        return jnp.broadcast_to(row, (8, 128))

    def as_column(row):
        return jnp.sum(jnp.where(diag, row[0:1, :], 0.0), axis=1, keepdims=True)

    ridge = ridge_ref[0]
    keys = kf[...]
    keys_b = keys.astype(BF16)
    group_row = lax.broadcasted_iota(jnp.int32, (GROUP, 1), 0) // draft

    groups = n // GROUP

    def group_product(dir_b, g, wait):
        lhs = dir_b[g * GROUP : (g + 1) * GROUP]
        acc = None
        for j in range(per_group):
            s = g * per_group + j
            if wait:
                cov_in[s].wait()
            prod = dot_nt(lhs, cov_v[s])
            acc = prod if acc is None else jnp.where(group_row == j, prod, acc)
        return decay[g * GROUP : (g + 1) * GROUP] * acc

    mine = pl.ds(pl.multiple_of(key * rows, 128), rows)
    direction = dref[...]
    rref[...] = direction
    sq_norm = jnp.sum(direction * direction, axis=1, keepdims=True)
    sends = []
    for it in range(ITERS - 1):
        dir_b = dref[...].astype(BF16)
        copies = []
        for g in range(groups):
            at = pl.ds(g * GROUP, GROUP)
            img[it, key, at, :] = group_product(dir_b, g, it == 0).astype(BF16)
            if it == 0 and g == 0:
                pl.semaphore_wait(barrier, n_key - 1 + n_head - 1)
            for d in range(1, n_key):
                c = pltpu.make_async_remote_copy(
                    src_ref=img.at[it, key, at],
                    dst_ref=img.at[it, key, at],
                    send_sem=img_ss.at[it, d, g],
                    recv_sem=img_rs.at[it, d, g],
                    device_id={"key": lax.rem(key + d, n_key)},
                    device_id_type=MESH,
                )
                c.start()
                copies.append(c)
        if it == 0:
            for c in vs_in + [w_in]:
                c.start()
        dots = dot_nt(dir_b, keys_b)
        bref[...] = dot_high(mix * dots, keys) + ridge * dref[...]
        for c in copies:
            c.wait_recv()
        sends += copies
        applied = jnp.concatenate([img[it, j].astype(F32) for j in range(n_key)], axis=1) + bref[...]
        direction = dref[...]
        step = sq_norm / jnp.sum(direction * applied, axis=1, keepdims=True)
        if it == 0:
            xref[...] = step * direction
        else:
            xref[...] = xref[...] + step * direction
        residual = rref[...] - step * applied
        rref[...] = residual
        new_norm = jnp.sum(residual * residual, axis=1, keepdims=True)
        dref[...] = residual + (new_norm / sq_norm) * direction
        sq_norm = new_norm

    dir_b = dref[...].astype(BF16)
    image = jnp.concatenate([group_product(dir_b, g, False) for g in range(groups)], axis=0)
    den_send[...] = as_row(jnp.sum(image * dref[:, mine], axis=1, keepdims=True))
    for d in range(1, n_key):
        c = pltpu.make_async_remote_copy(
            src_ref=den_send,
            dst_ref=den_recv.at[d],
            send_sem=den_ss.at[d],
            recv_sem=den_rs.at[d],
            device_id={"key": lax.rem(key + d, n_key)},
            device_id_type=MESH,
        )
        c.start()
        sends.append(c)
    dens = sends[-(n_key - 1) :]

    x_rows = xref[:, mine].astype(BF16)
    d_rows = dref[:, mine].astype(BF16)
    reads = []
    for g in range(groups):
        at = slice(g * GROUP, (g + 1) * GROUP)
        lhs = jnp.concatenate([x_rows[at], d_rows[at]], axis=0)
        acc_x = acc_d = None
        for j in range(per_group):
            s = g * per_group + j
            vs_in[s].wait()
            prod = dot_nt(lhs, vs_v[s])
            px, pd = prod[:GROUP], prod[GROUP:]
            acc_x = px if acc_x is None else jnp.where(group_row == j, px, acc_x)
            acc_d = pd if acc_d is None else jnp.where(group_row == j, pd, acc_d)
        acc_x = (decay[at] * acc_x).astype(BF16)
        acc_d = (decay[at] * acc_d).astype(BF16)
        for j in range(n_key):
            cols = slice(j * vcols, (j + 1) * vcols)
            rd_send[g, j, 0] = acc_x[:, cols]
            rd_send[g, j, 1] = acc_d[:, cols]
        for d in range(1, n_key):
            to = lax.rem(key + d, n_key)
            c = pltpu.make_async_remote_copy(
                src_ref=rd_send.at[g, to],
                dst_ref=rd_recv.at[g, d],
                send_sem=rd_ss.at[g, d],
                recv_sem=rd_rs.at[g, d],
                device_id={"key": to},
                device_id_type=MESH,
            )
            c.start()
            reads.append(c)
    sends += reads
    dots_d = dot_nt(dir_b, keys_b)
    dots_x = dot_nt(xref[...].astype(BF16), keys_b)
    base = dot_high(mix * dots_d, keys) + ridge * dref[...]
    den = jnp.sum(base * dref[...], axis=1, keepdims=True) + as_column(den_send[...])
    vcol = pl.ds(pl.multiple_of(key * vcols, 128), vcols)
    vals = vf[:, vcol]

    def stacked(ref, slot, part):
        return jnp.concatenate([ref[g, slot, part].astype(F32) for g in range(groups)], axis=0)

    read_x = dot_high(mix * dots_x, vals) + stacked(rd_send, key, 0)
    read_d = dot_high(mix * dots_d, vals) + stacked(rd_send, key, 1)
    for d in range(1, n_key):
        dens[d - 1].wait_recv()
        den = den + as_column(den_recv[d])
    step = sq_norm / den
    for c in reads:
        c.wait_recv()
    for d in range(1, n_key):
        read_x = read_x + stacked(rd_recv, d, 0)
        read_d = read_d + stacked(rd_recv, d, 1)
    read = read_x + step * read_d

    sq_send[...] = as_row(jnp.sum(read * read, axis=1, keepdims=True))
    squares = []
    for d in range(1, n_key):
        c = pltpu.make_async_remote_copy(
            src_ref=sq_send,
            dst_ref=sq_recv.at[d],
            send_sem=sq_ss.at[d],
            recv_sem=sq_rs.at[d],
            device_id={"key": lax.rem(key + d, n_key)},
            device_id_type=MESH,
        )
        c.start()
        squares.append(c)
    sends += squares
    gained = (read * gain_v[...]).astype(BF16)
    w_in.wait()

    core = lax.rem(key, 2)
    chip = key // 2
    partner = key + 1 - 2 * core
    across = lax.rem(key + 2, n_key)

    def project(to_key, to_head):
        at = pl.multiple_of((to_key * n_head + to_head) * block, 128)
        return jnp.dot(gained, w_v[:, pl.ds(at, block)], preferred_element_type=F32)

    order = list(range(1, n_head)) + [0]
    core_copy, x_copy, z_copy = {}, {}, {}
    scale = []

    def stage_a(o):
        to = lax.rem(head + o, n_head)
        for half in range(2):
            core_send[o, half] = project(2 * half + 1 - core, to).astype(BF16)
        c = pltpu.make_async_remote_copy(
            src_ref=core_send.at[o],
            dst_ref=core_recv.at[o],
            send_sem=core_ss.at[o],
            recv_sem=core_rs.at[o],
            device_id={"key": partner},
            device_id_type=MESH,
        )
        c.start()
        core_copy[o] = c
        for half in range(2):
            own[o, half] = project(2 * half + core, to)

    def stage_b(o):
        core_copy[o].wait_recv()
        other = 1 - chip
        x_send[o] = (own[o, other] + core_recv[o, other].astype(F32)).astype(BF16)
        c = pltpu.make_async_remote_copy(
            src_ref=x_send.at[o],
            dst_ref=x_recv.at[o],
            send_sem=x_ss.at[o],
            recv_sem=x_rs.at[o],
            device_id={"key": across},
            device_id_type=MESH,
        )
        c.start()
        x_copy[o] = c
        keep[o] = own[o, chip] + core_recv[o, chip].astype(F32)

    def stage_c(o):
        if not scale:
            total = as_column(sq_send[...])
            for d in range(1, n_key):
                squares[d - 1].wait_recv()
                total = total + as_column(sq_recv[d])
            scale.append(lax.rsqrt(total / values + 1e-06))
        x_copy[o].wait_recv()
        done = (keep[o] + x_recv[o].astype(F32)) * scale[0]
        if o == 0:
            keep[o] = done
            return
        z_send[o] = done.astype(BF16)
        c = pltpu.make_async_remote_copy(
            src_ref=z_send.at[o],
            dst_ref=z_recv.at[o],
            send_sem=z_ss.at[o],
            recv_sem=z_rs.at[o],
            device_id={"head": lax.rem(head + o, n_head)},
            device_id_type=MESH,
        )
        c.start()
        z_copy[o] = c

    for i in range(n_head + 2):
        if i < n_head:
            stage_a(order[i])
        if 0 <= i - 1 < n_head:
            stage_b(order[i - 1])
        if 0 <= i - 2 < n_head:
            stage_c(order[i - 2])
    result = keep[0]
    for o in range(1, n_head):
        z_copy[o].wait_recv()
        result = result + z_recv[o].astype(F32)
    keep[0] = result
    for s in range(seqs):
        out_ref[s] = keep[0, s * draft : (s + 1) * draft, :].astype(BF16)
    for c in sends + list(core_copy.values()) + list(x_copy.values()) + list(z_copy.values()):
        c.wait_send()


def solution(mesh):
    n_key, n_head = mesh.shape["key"], mesh.shape["head"]
    assert n_key == 4

    def body(q, k, v, dg, wg, ridge, gain, cov, vs, w):
        seqs, _, draft, width = q.shape
        rows = cov.shape[2]
        values = vs.shape[2]
        vcols = values // n_key
        model = w.shape[2]
        block = model // (n_key * n_head)
        n = seqs * draft
        dma = pltpu.SemaphoreType.DMA
        out = pl.pallas_call(
            functools.partial(kernel, n_key, n_head),
            out_shape=jax.ShapeDtypeStruct((seqs, draft, block), BF16),
            in_specs=[pl.BlockSpec(memory_space=pl.ANY)] * 5
            + [pl.BlockSpec(memory_space=pltpu.SMEM)]
            + [pl.BlockSpec(memory_space=pl.ANY)] * 4,
            out_specs=pl.BlockSpec(memory_space=pltpu.VMEM),
            scratch_shapes=[
                pltpu.VMEM((seqs, draft, width), BF16),
                pltpu.VMEM((seqs, draft, width), BF16),
                pltpu.VMEM((seqs, draft, values), BF16),
                pltpu.VMEM((1, draft, seqs), F32),
                pltpu.VMEM((1, draft, seqs), F32),
                pltpu.VMEM(gain.shape, F32),
                pltpu.VMEM((seqs, rows, width), BF16),
                pltpu.VMEM((seqs, values, rows), BF16),
                pltpu.VMEM(w.shape[1:], BF16),
                pltpu.VMEM((n, width), F32),
                pltpu.VMEM((n, values), F32),
                pltpu.VMEM((n, width), F32),
                pltpu.VMEM((n, width), F32),
                pltpu.VMEM((n, width), F32),
                pltpu.VMEM((n, width), F32),
                pltpu.VMEM((ITERS - 1, n_key, n, rows), BF16),
                pltpu.VMEM((n // GROUP, n_key, 2, GROUP, vcols), BF16),
                pltpu.VMEM((n // GROUP, n_key, 2, GROUP, vcols), BF16),
                pltpu.VMEM((8, 128), F32),
                pltpu.VMEM((n_key, 8, 128), F32),
                pltpu.VMEM((8, 128), F32),
                pltpu.VMEM((n_key, 8, 128), F32),
                pltpu.VMEM((n_head, 2, n, block), BF16),
                pltpu.VMEM((n_head, 2, n, block), BF16),
                pltpu.VMEM((n_head, 2, n, block), F32),
                pltpu.VMEM((n_head, n, block), BF16),
                pltpu.VMEM((n_head, n, block), BF16),
                pltpu.VMEM((n_head, n, block), F32),
                pltpu.VMEM((n_head, n, block), BF16),
                pltpu.VMEM((n_head, n, block), BF16),
                dma((6,)),
                dma((seqs,)),
                dma((seqs,)),
                dma,
                dma((ITERS - 1, n_key, n // GROUP)),
                dma((ITERS - 1, n_key, n // GROUP)),
                dma((n // GROUP, n_key)),
                dma((n // GROUP, n_key)),
                dma((n_key,)),
                dma((n_key,)),
                dma((n_key,)),
                dma((n_key,)),
                dma((n_head,)),
                dma((n_head,)),
                dma((n_head,)),
                dma((n_head,)),
                dma((n_head,)),
                dma((n_head,)),
            ],
            compiler_params=pltpu.CompilerParams(collective_id=0, has_side_effects=True),
        )(
            q,
            k,
            v,
            dg.transpose(1, 2, 0),
            wg.transpose(1, 2, 0),
            ridge,
            gain,
            cov,
            vs,
            w,
        )
        return out

    placed = (
        P("batch", "head", None, None),
        P("batch", "head", None, None),
        P("batch", "head", None, None),
        P("batch", "head", None),
        P("batch", "head", None),
        P("head"),
        P("head", "key"),
        P("batch", "head", "key", None),
        P("batch", "head", None, "key"),
        P("head", "key", None),
    )
    return jax.shard_map(
        body,
        mesh=mesh,
        in_specs=placed,
        out_specs=P("batch", None, ("key", "head")),
        check_vma=False,
    )
```

```python
import functools

import jax
import jax.numpy as jnp
from jax import lax
from jax.experimental import pallas as pl
from jax.experimental.pallas import tpu as pltpu
from jax.sharding import PartitionSpec as P

ITERS = 3
MESH = pl.DeviceIdType.MESH
F32 = jnp.float32
BF16 = jnp.bfloat16
HIGH = lax.Precision.HIGHEST
GROUP = 16


def dot_nt(a, b):
    return lax.dot_general(a, b, (((1,), (1,)), ((), ())), preferred_element_type=F32)


def dot_high(a, b):
    return lax.dot_general(
        a, b, (((1,), (0,)), ((), ())), precision=HIGH, preferred_element_type=F32
    )


def kernel(
    n_key,
    n_head,
    q_h,
    k_h,
    v_h,
    dg_h,
    wg_h,
    ridge_ref,
    gain_h,
    cov_h,
    vs_h,
    w_h,
    out_ref,
    q_v,
    k_v,
    v_v,
    dg_v,
    wg_v,
    gain_v,
    cov_v,
    vs_v,
    w_v,
    kf,
    vf,
    dref,
    rref,
    xref,
    bref,
    img,
    rd_send,
    rd_recv,
    den_send,
    den_recv,
    sq_send,
    sq_recv,
    core_send,
    core_recv,
    own,
    x_send,
    x_recv,
    keep,
    z_send,
    z_recv,
    in_sem,
    cov_sem,
    vs_sem,
    w_sem,
    img_ss,
    img_rs,
    rd_ss,
    rd_rs,
    den_ss,
    den_rs,
    sq_ss,
    sq_rs,
    core_ss,
    core_rs,
    x_ss,
    x_rs,
    z_ss,
    z_rs,
):
    key = lax.axis_index("key")
    head = lax.axis_index("head")
    seqs, draft, width = q_v.shape
    rows = cov_v.shape[1]
    values = vs_v.shape[1]
    vcols = values // n_key
    n = seqs * draft
    block = out_ref.shape[2]
    per_group = GROUP // draft

    barrier = pltpu.get_barrier_semaphore()
    for d in range(1, n_key):
        pl.semaphore_signal(
            barrier, inc=1, device_id={"key": lax.rem(key + d, n_key)}, device_id_type=MESH
        )
    for d in range(1, n_head):
        pl.semaphore_signal(
            barrier, inc=1, device_id={"head": lax.rem(head + d, n_head)}, device_id_type=MESH
        )

    small = []
    pairs = ((q_h.at[:, 0], q_v), (k_h.at[:, 0], k_v), (dg_h, dg_v), (wg_h, wg_v), (v_h.at[:, 0], v_v), (gain_h, gain_v))
    for i, (src, dst) in enumerate(pairs):
        small.append(pltpu.make_async_copy(src, dst, in_sem.at[i]))
    cov_in = [pltpu.make_async_copy(cov_h.at[s, 0], cov_v.at[s], cov_sem.at[s]) for s in range(seqs)]
    vs_in = [pltpu.make_async_copy(vs_h.at[s, 0], vs_v.at[s], vs_sem.at[s]) for s in range(seqs)]
    w_in = pltpu.make_async_copy(w_h.at[0], w_v, w_sem)
    for c in small + cov_in:
        c.start()
    for c in small:
        c.wait()

    for s in range(seqs):
        at = pl.ds(s * draft, draft)
        dref[at, :] = q_v[s].astype(F32)
        kf[at, :] = k_v[s].astype(F32)
        vf[at, :] = v_v[s].astype(F32)

    row_id = lax.broadcasted_iota(jnp.int32, (n, 1), 0)
    tok = lax.rem(row_id, draft)
    first = row_id - tok
    seq_hot = lax.broadcasted_iota(jnp.int32, (n, seqs), 1) == row_id // draft

    def per_row(gates, u):
        return jnp.sum(jnp.where(seq_hot, gates[u : u + 1, :], 0.0), axis=1, keepdims=True)

    gates, writes = dg_v[0], wg_v[0]
    totals = [per_row(gates, 0)]
    for u in range(1, draft):
        totals.append(totals[-1] * per_row(gates, u))
    decay = totals[0]
    for u in range(1, draft):
        decay = jnp.where(tok == u, totals[u], decay)
    col_id = lax.broadcasted_iota(jnp.int32, (n, n), 1)
    mix = jnp.zeros((n, n), F32)
    for u in range(draft):
        weight = per_row(writes, u) * (decay / totals[u])
        mix = jnp.where((col_id == first + u) & (tok >= u), weight, mix)
    lane = lax.broadcasted_iota(jnp.int32, (n, 128), 1)
    diag = lane == lax.broadcasted_iota(jnp.int32, (n, 128), 0)

    def as_row(column):
        row = jnp.sum(jnp.where(diag, column, 0.0), axis=0, keepdims=True)
        return jnp.broadcast_to(row, (8, 128))

    def as_column(row):
        return jnp.sum(jnp.where(diag, row[0:1, :], 0.0), axis=1, keepdims=True)

    ridge = ridge_ref[0]
    keys = kf[...]
    keys_b = keys.astype(BF16)
    group_row = lax.broadcasted_iota(jnp.int32, (GROUP, 1), 0) // draft

    groups = n // GROUP

    def group_product(dir_b, g, wait):
        lhs = dir_b[g * GROUP : (g + 1) * GROUP]
        acc = None
        for j in range(per_group):
            s = g * per_group + j
            if wait:
                cov_in[s].wait()
            prod = dot_nt(lhs, cov_v[s])
            acc = prod if acc is None else jnp.where(group_row == j, prod, acc)
        return decay[g * GROUP : (g + 1) * GROUP] * acc

    mine = pl.ds(pl.multiple_of(key * rows, 128), rows)
    direction = dref[...]
    rref[...] = direction
    sq_norm = jnp.sum(direction * direction, axis=1, keepdims=True)
    sends = []
    for it in range(ITERS - 1):
        dir_b = dref[...].astype(BF16)
        copies = []
        for g in range(groups):
            at = pl.ds(g * GROUP, GROUP)
            img[it, key, at, :] = group_product(dir_b, g, it == 0).astype(BF16)
            if it == 0 and g == 0:
                pl.semaphore_wait(barrier, n_key - 1 + n_head - 1)
            for d in range(1, n_key):
                c = pltpu.make_async_remote_copy(
                    src_ref=img.at[it, key, at],
                    dst_ref=img.at[it, key, at],
                    send_sem=img_ss.at[it, d, g],
                    recv_sem=img_rs.at[it, d, g],
                    device_id={"key": lax.rem(key + d, n_key)},
                    device_id_type=MESH,
                )
                c.start()
                copies.append(c)
        if it == 0:
            for c in vs_in + [w_in]:
                c.start()
        dots = dot_nt(dir_b, keys_b)
        bref[...] = dot_high(mix * dots, keys) + ridge * dref[...]
        for c in copies:
            c.wait_recv()
        sends += copies
        applied = jnp.concatenate([img[it, j].astype(F32) for j in range(n_key)], axis=1) + bref[...]
        direction = dref[...]
        step = sq_norm / jnp.sum(direction * applied, axis=1, keepdims=True)
        if it == 0:
            xref[...] = step * direction
        else:
            xref[...] = xref[...] + step * direction
        residual = rref[...] - step * applied
        rref[...] = residual
        new_norm = jnp.sum(residual * residual, axis=1, keepdims=True)
        dref[...] = residual + (new_norm / sq_norm) * direction
        sq_norm = new_norm

    dir_b = dref[...].astype(BF16)
    x_rows = xref[:, mine].astype(BF16)
    d_rows = dref[:, mine].astype(BF16)
    reads = []
    for g in range(groups):
        at = slice(g * GROUP, (g + 1) * GROUP)
        lhs = jnp.concatenate([x_rows[at], d_rows[at]], axis=0)
        acc_x = acc_d = None
        for j in range(per_group):
            s = g * per_group + j
            vs_in[s].wait()
            prod = dot_nt(lhs, vs_v[s])
            px, pd = prod[:GROUP], prod[GROUP:]
            acc_x = px if acc_x is None else jnp.where(group_row == j, px, acc_x)
            acc_d = pd if acc_d is None else jnp.where(group_row == j, pd, acc_d)
        acc_x = (decay[at] * acc_x).astype(BF16)
        acc_d = (decay[at] * acc_d).astype(BF16)
        for j in range(n_key):
            cols = slice(j * vcols, (j + 1) * vcols)
            rd_send[g, j, 0] = acc_x[:, cols]
            rd_send[g, j, 1] = acc_d[:, cols]
        for d in range(1, n_key):
            to = lax.rem(key + d, n_key)
            c = pltpu.make_async_remote_copy(
                src_ref=rd_send.at[g, to],
                dst_ref=rd_recv.at[g, d],
                send_sem=rd_ss.at[g, d],
                recv_sem=rd_rs.at[g, d],
                device_id={"key": to},
                device_id_type=MESH,
            )
            c.start()
            reads.append(c)
    sends += reads
    image = jnp.concatenate([group_product(dir_b, g, False) for g in range(groups)], axis=0)
    den_send[...] = as_row(jnp.sum(image * dref[:, mine], axis=1, keepdims=True))
    for d in range(1, n_key):
        c = pltpu.make_async_remote_copy(
            src_ref=den_send,
            dst_ref=den_recv.at[d],
            send_sem=den_ss.at[d],
            recv_sem=den_rs.at[d],
            device_id={"key": lax.rem(key + d, n_key)},
            device_id_type=MESH,
        )
        c.start()
        sends.append(c)
    dens = sends[-(n_key - 1) :]

    dots_d = dot_nt(dir_b, keys_b)
    dots_x = dot_nt(xref[...].astype(BF16), keys_b)
    base = dot_high(mix * dots_d, keys) + ridge * dref[...]
    den = jnp.sum(base * dref[...], axis=1, keepdims=True) + as_column(den_send[...])
    vcol = pl.ds(pl.multiple_of(key * vcols, 128), vcols)
    vals = vf[:, vcol]

    def stacked(ref, slot, part):
        return jnp.concatenate([ref[g, slot, part].astype(F32) for g in range(groups)], axis=0)

    read_x = dot_high(mix * dots_x, vals) + stacked(rd_send, key, 0)
    read_d = dot_high(mix * dots_d, vals) + stacked(rd_send, key, 1)
    for d in range(1, n_key):
        dens[d - 1].wait_recv()
        den = den + as_column(den_recv[d])
    step = sq_norm / den
    for c in reads:
        c.wait_recv()
    for d in range(1, n_key):
        read_x = read_x + stacked(rd_recv, d, 0)
        read_d = read_d + stacked(rd_recv, d, 1)
    read = read_x + step * read_d

    sq_send[...] = as_row(jnp.sum(read * read, axis=1, keepdims=True))
    squares = []
    for d in range(1, n_key):
        c = pltpu.make_async_remote_copy(
            src_ref=sq_send,
            dst_ref=sq_recv.at[d],
            send_sem=sq_ss.at[d],
            recv_sem=sq_rs.at[d],
            device_id={"key": lax.rem(key + d, n_key)},
            device_id_type=MESH,
        )
        c.start()
        squares.append(c)
    sends += squares
    gained = (read * gain_v[...]).astype(BF16)
    w_in.wait()

    core = lax.rem(key, 2)
    chip = key // 2
    partner = key + 1 - 2 * core
    across = lax.rem(key + 2, n_key)

    def project(to_key, to_head):
        at = pl.multiple_of((to_key * n_head + to_head) * block, 128)
        return jnp.dot(gained, w_v[:, pl.ds(at, block)], preferred_element_type=F32)

    order = sorted(range(1, n_head), key=lambda o: abs(2 * o - n_head)) + [0]
    core_copy, x_copy, z_copy = {}, {}, {}
    scale = []

    def stage_a(o):
        to = lax.rem(head + o, n_head)
        core_copy[o] = []
        for part, side in enumerate((1 - chip, chip)):
            core_send[o, part] = project(2 * side + 1 - core, to).astype(BF16)
            c = pltpu.make_async_remote_copy(
                src_ref=core_send.at[o, part],
                dst_ref=core_recv.at[o, part],
                send_sem=core_ss.at[o, part],
                recv_sem=core_rs.at[o, part],
                device_id={"key": partner},
                device_id_type=MESH,
            )
            c.start()
            core_copy[o].append(c)
        for part, side in enumerate((1 - chip, chip)):
            own[o, part] = project(2 * side + core, to)

    def stage_b(o):
        core_copy[o][0].wait_recv()
        x_send[o] = (own[o, 0] + core_recv[o, 0].astype(F32)).astype(BF16)
        c = pltpu.make_async_remote_copy(
            src_ref=x_send.at[o],
            dst_ref=x_recv.at[o],
            send_sem=x_ss.at[o],
            recv_sem=x_rs.at[o],
            device_id={"key": across},
            device_id_type=MESH,
        )
        c.start()
        x_copy[o] = c
        core_copy[o][1].wait_recv()
        keep[o] = own[o, 1] + core_recv[o, 1].astype(F32)

    def stage_c(o):
        if not scale:
            total = as_column(sq_send[...])
            for d in range(1, n_key):
                squares[d - 1].wait_recv()
                total = total + as_column(sq_recv[d])
            scale.append(lax.rsqrt(total / values + 1e-06))
        x_copy[o].wait_recv()
        done = (keep[o] + x_recv[o].astype(F32)) * scale[0]
        if o == 0:
            keep[o] = done
            return
        z_send[o] = done.astype(BF16)
        c = pltpu.make_async_remote_copy(
            src_ref=z_send.at[o],
            dst_ref=z_recv.at[o],
            send_sem=z_ss.at[o],
            recv_sem=z_rs.at[o],
            device_id={"head": lax.rem(head + o, n_head)},
            device_id_type=MESH,
        )
        c.start()
        z_copy[o] = c

    for i in range(n_head + 2):
        if i < n_head:
            stage_a(order[i])
        if 0 <= i - 1 < n_head:
            stage_b(order[i - 1])
        if 0 <= i - 2 < n_head:
            stage_c(order[i - 2])
    result = keep[0]
    for o in range(1, n_head):
        z_copy[o].wait_recv()
        result = result + z_recv[o].astype(F32)
    keep[0] = result
    for s in range(seqs):
        out_ref[s] = keep[0, s * draft : (s + 1) * draft, :].astype(BF16)
    for c in sends + [c for pair in core_copy.values() for c in pair] + list(x_copy.values()) + list(z_copy.values()):
        c.wait_send()


def solution(mesh):
    n_key, n_head = mesh.shape["key"], mesh.shape["head"]
    assert n_key == 4

    def body(q, k, v, dg, wg, ridge, gain, cov, vs, w):
        seqs, _, draft, width = q.shape
        rows = cov.shape[2]
        values = vs.shape[2]
        vcols = values // n_key
        model = w.shape[2]
        block = model // (n_key * n_head)
        n = seqs * draft
        dma = pltpu.SemaphoreType.DMA
        out = pl.pallas_call(
            functools.partial(kernel, n_key, n_head),
            out_shape=jax.ShapeDtypeStruct((seqs, draft, block), BF16),
            in_specs=[pl.BlockSpec(memory_space=pl.ANY)] * 5
            + [pl.BlockSpec(memory_space=pltpu.SMEM)]
            + [pl.BlockSpec(memory_space=pl.ANY)] * 4,
            out_specs=pl.BlockSpec(memory_space=pltpu.VMEM),
            scratch_shapes=[
                pltpu.VMEM((seqs, draft, width), BF16),
                pltpu.VMEM((seqs, draft, width), BF16),
                pltpu.VMEM((seqs, draft, values), BF16),
                pltpu.VMEM((1, draft, seqs), F32),
                pltpu.VMEM((1, draft, seqs), F32),
                pltpu.VMEM(gain.shape, F32),
                pltpu.VMEM((seqs, rows, width), BF16),
                pltpu.VMEM((seqs, values, rows), BF16),
                pltpu.VMEM(w.shape[1:], BF16),
                pltpu.VMEM((n, width), F32),
                pltpu.VMEM((n, values), F32),
                pltpu.VMEM((n, width), F32),
                pltpu.VMEM((n, width), F32),
                pltpu.VMEM((n, width), F32),
                pltpu.VMEM((n, width), F32),
                pltpu.VMEM((ITERS - 1, n_key, n, rows), BF16),
                pltpu.VMEM((n // GROUP, n_key, 2, GROUP, vcols), BF16),
                pltpu.VMEM((n // GROUP, n_key, 2, GROUP, vcols), BF16),
                pltpu.VMEM((8, 128), F32),
                pltpu.VMEM((n_key, 8, 128), F32),
                pltpu.VMEM((8, 128), F32),
                pltpu.VMEM((n_key, 8, 128), F32),
                pltpu.VMEM((n_head, 2, n, block), BF16),
                pltpu.VMEM((n_head, 2, n, block), BF16),
                pltpu.VMEM((n_head, 2, n, block), F32),
                pltpu.VMEM((n_head, n, block), BF16),
                pltpu.VMEM((n_head, n, block), BF16),
                pltpu.VMEM((n_head, n, block), F32),
                pltpu.VMEM((n_head, n, block), BF16),
                pltpu.VMEM((n_head, n, block), BF16),
                dma((6,)),
                dma((seqs,)),
                dma((seqs,)),
                dma,
                dma((ITERS - 1, n_key, n // GROUP)),
                dma((ITERS - 1, n_key, n // GROUP)),
                dma((n // GROUP, n_key)),
                dma((n // GROUP, n_key)),
                dma((n_key,)),
                dma((n_key,)),
                dma((n_key,)),
                dma((n_key,)),
                dma((n_head, 2)),
                dma((n_head, 2)),
                dma((n_head,)),
                dma((n_head,)),
                dma((n_head,)),
                dma((n_head,)),
            ],
            compiler_params=pltpu.CompilerParams(collective_id=0, has_side_effects=True),
        )(
            q,
            k,
            v,
            dg.transpose(1, 2, 0),
            wg.transpose(1, 2, 0),
            ridge,
            gain,
            cov,
            vs,
            w,
        )
        return out

    placed = (
        P("batch", "head", None, None),
        P("batch", "head", None, None),
        P("batch", "head", None, None),
        P("batch", "head", None),
        P("batch", "head", None),
        P("head"),
        P("head", "key"),
        P("batch", "head", "key", None),
        P("batch", "head", None, "key"),
        P("head", "key", None),
    )
    return jax.shard_map(
        body,
        mesh=mesh,
        in_specs=placed,
        out_specs=P("batch", None, ("key", "head")),
        check_vma=False,
    )
```

```python
import functools

import jax
import jax.numpy as jnp
from jax import lax
from jax.experimental import pallas as pl
from jax.experimental.pallas import tpu as pltpu
from jax.sharding import PartitionSpec as P

ITERS = 3
MESH = pl.DeviceIdType.MESH
F32 = jnp.float32
BF16 = jnp.bfloat16
GROUP = 16


def dot_nt(a, b):
    return lax.dot_general(a, b, (((1,), (1,)), ((), ())), preferred_element_type=F32)


def dot_split(a, b):
    top = a.astype(BF16)
    rest = a - top.astype(F32)
    middle = rest.astype(BF16)
    low = (rest - middle.astype(F32)).astype(BF16)
    m = a.shape[0]
    parts = jnp.dot(
        jnp.concatenate([top, middle, low], axis=0), b, preferred_element_type=F32
    )
    return parts[:m] + (parts[m : 2 * m] + parts[2 * m :])


def kernel(
    n_key,
    n_head,
    q_h,
    k_h,
    v_h,
    dg_h,
    wg_h,
    ridge_ref,
    gain_h,
    cov_h,
    vs_h,
    w_h,
    out_ref,
    q_v,
    k_v,
    v_v,
    dg_v,
    wg_v,
    gain_v,
    cov_v,
    vs_v,
    w_v,
    kf,
    vf,
    dref,
    rref,
    xref,
    bref,
    img,
    rd_send,
    rd_recv,
    den_send,
    den_recv,
    sq_send,
    sq_recv,
    core_send,
    core_recv,
    own,
    x_send,
    x_recv,
    keep,
    z_send,
    z_recv,
    in_sem,
    cov_sem,
    vs_sem,
    w_sem,
    img_ss,
    img_rs,
    rd_ss,
    rd_rs,
    den_ss,
    den_rs,
    sq_ss,
    sq_rs,
    core_ss,
    core_rs,
    x_ss,
    x_rs,
    z_ss,
    z_rs,
):
    key = lax.axis_index("key")
    head = lax.axis_index("head")
    seqs, draft, width = q_v.shape
    rows = cov_v.shape[1]
    values = vs_v.shape[1]
    vcols = values // n_key
    n = seqs * draft
    block = out_ref.shape[2]
    per_group = GROUP // draft

    barrier = pltpu.get_barrier_semaphore()
    for d in range(1, n_key):
        pl.semaphore_signal(
            barrier, inc=1, device_id={"key": lax.rem(key + d, n_key)}, device_id_type=MESH
        )
    for d in range(1, n_head):
        pl.semaphore_signal(
            barrier, inc=1, device_id={"head": lax.rem(head + d, n_head)}, device_id_type=MESH
        )

    small = []
    pairs = ((q_h.at[:, 0], q_v), (k_h.at[:, 0], k_v), (dg_h, dg_v), (wg_h, wg_v), (v_h.at[:, 0], v_v), (gain_h, gain_v))
    for i, (src, dst) in enumerate(pairs):
        small.append(pltpu.make_async_copy(src, dst, in_sem.at[i]))
    cov_in = [pltpu.make_async_copy(cov_h.at[s, 0], cov_v.at[s], cov_sem.at[s]) for s in range(seqs)]
    vs_in = [pltpu.make_async_copy(vs_h.at[s, 0], vs_v.at[s], vs_sem.at[s]) for s in range(seqs)]
    w_in = pltpu.make_async_copy(w_h.at[0], w_v, w_sem)
    for c in small + cov_in:
        c.start()
    for c in small:
        c.wait()

    for s in range(seqs):
        at = pl.ds(s * draft, draft)
        dref[at, :] = q_v[s].astype(F32)
        kf[at, :] = k_v[s].astype(F32)
        vf[at, :] = v_v[s].astype(F32)

    row_id = lax.broadcasted_iota(jnp.int32, (n, 1), 0)
    tok = lax.rem(row_id, draft)
    first = row_id - tok
    seq_hot = lax.broadcasted_iota(jnp.int32, (n, seqs), 1) == row_id // draft

    def per_row(gates, u):
        return jnp.sum(jnp.where(seq_hot, gates[u : u + 1, :], 0.0), axis=1, keepdims=True)

    gates, writes = dg_v[0], wg_v[0]
    totals = [per_row(gates, 0)]
    for u in range(1, draft):
        totals.append(totals[-1] * per_row(gates, u))
    decay = totals[0]
    for u in range(1, draft):
        decay = jnp.where(tok == u, totals[u], decay)
    col_id = lax.broadcasted_iota(jnp.int32, (n, n), 1)
    mix = jnp.zeros((n, n), F32)
    for u in range(draft):
        weight = per_row(writes, u) * (decay / totals[u])
        mix = jnp.where((col_id == first + u) & (tok >= u), weight, mix)
    lane = lax.broadcasted_iota(jnp.int32, (n, 128), 1)
    diag = lane == lax.broadcasted_iota(jnp.int32, (n, 128), 0)

    def as_row(column):
        row = jnp.sum(jnp.where(diag, column, 0.0), axis=0, keepdims=True)
        return jnp.broadcast_to(row, (8, 128))

    def as_column(row):
        return jnp.sum(jnp.where(diag, row[0:1, :], 0.0), axis=1, keepdims=True)

    ridge = ridge_ref[0]
    keys = kf[...]
    keys_b = keys.astype(BF16)
    group_row = lax.broadcasted_iota(jnp.int32, (GROUP, 1), 0) // draft

    groups = n // GROUP

    def group_product(dir_b, g, wait):
        lhs = dir_b[g * GROUP : (g + 1) * GROUP]
        acc = None
        for j in range(per_group):
            s = g * per_group + j
            if wait:
                cov_in[s].wait()
            prod = dot_nt(lhs, cov_v[s])
            acc = prod if acc is None else jnp.where(group_row == j, prod, acc)
        return decay[g * GROUP : (g + 1) * GROUP] * acc

    mine = pl.ds(pl.multiple_of(key * rows, 128), rows)
    direction = dref[...]
    rref[...] = direction
    sq_norm = jnp.sum(direction * direction, axis=1, keepdims=True)
    sends = []
    for it in range(ITERS - 1):
        dir_b = dref[...].astype(BF16)
        copies = []
        for g in range(groups):
            at = pl.ds(g * GROUP, GROUP)
            img[it, key, at, :] = group_product(dir_b, g, it == 0).astype(BF16)
            if it == 0 and g == 0:
                pl.semaphore_wait(barrier, n_key - 1 + n_head - 1)
            for d in range(1, n_key):
                c = pltpu.make_async_remote_copy(
                    src_ref=img.at[it, key, at],
                    dst_ref=img.at[it, key, at],
                    send_sem=img_ss.at[it, d, g],
                    recv_sem=img_rs.at[it, d, g],
                    device_id={"key": lax.rem(key + d, n_key)},
                    device_id_type=MESH,
                )
                c.start()
                copies.append(c)
        if it == 0:
            for c in vs_in + [w_in]:
                c.start()
        dots = dot_nt(dir_b, keys_b)
        bref[...] = dot_split(mix * dots, keys_b) + ridge * dref[...]
        for c in copies:
            c.wait_recv()
        sends += copies
        applied = jnp.concatenate([img[it, j].astype(F32) for j in range(n_key)], axis=1) + bref[...]
        direction = dref[...]
        step = sq_norm / jnp.sum(direction * applied, axis=1, keepdims=True)
        if it == 0:
            xref[...] = step * direction
        else:
            xref[...] = xref[...] + step * direction
        residual = rref[...] - step * applied
        rref[...] = residual
        new_norm = jnp.sum(residual * residual, axis=1, keepdims=True)
        dref[...] = residual + (new_norm / sq_norm) * direction
        sq_norm = new_norm

    dir_b = dref[...].astype(BF16)
    x_rows = xref[:, mine].astype(BF16)
    d_rows = dref[:, mine].astype(BF16)
    reads = []
    for g in range(groups):
        at = slice(g * GROUP, (g + 1) * GROUP)
        lhs = jnp.concatenate([x_rows[at], d_rows[at]], axis=0)
        acc_x = acc_d = None
        for j in range(per_group):
            s = g * per_group + j
            vs_in[s].wait()
            prod = dot_nt(lhs, vs_v[s])
            px, pd = prod[:GROUP], prod[GROUP:]
            acc_x = px if acc_x is None else jnp.where(group_row == j, px, acc_x)
            acc_d = pd if acc_d is None else jnp.where(group_row == j, pd, acc_d)
        acc_x = (decay[at] * acc_x).astype(BF16)
        acc_d = (decay[at] * acc_d).astype(BF16)
        for j in range(n_key):
            cols = slice(j * vcols, (j + 1) * vcols)
            rd_send[g, j, 0] = acc_x[:, cols]
            rd_send[g, j, 1] = acc_d[:, cols]
        for d in range(1, n_key):
            to = lax.rem(key + d, n_key)
            c = pltpu.make_async_remote_copy(
                src_ref=rd_send.at[g, to],
                dst_ref=rd_recv.at[g, d],
                send_sem=rd_ss.at[g, d],
                recv_sem=rd_rs.at[g, d],
                device_id={"key": to},
                device_id_type=MESH,
            )
            c.start()
            reads.append(c)
    sends += reads
    image = jnp.concatenate([group_product(dir_b, g, False) for g in range(groups)], axis=0)
    den_send[...] = as_row(jnp.sum(image * dref[:, mine], axis=1, keepdims=True))
    for d in range(1, n_key):
        c = pltpu.make_async_remote_copy(
            src_ref=den_send,
            dst_ref=den_recv.at[d],
            send_sem=den_ss.at[d],
            recv_sem=den_rs.at[d],
            device_id={"key": lax.rem(key + d, n_key)},
            device_id_type=MESH,
        )
        c.start()
        sends.append(c)
    dens = sends[-(n_key - 1) :]

    dots_d = dot_nt(dir_b, keys_b)
    dots_x = dot_nt(xref[...].astype(BF16), keys_b)
    base = dot_split(mix * dots_d, keys_b) + ridge * dref[...]
    den = jnp.sum(base * dref[...], axis=1, keepdims=True) + as_column(den_send[...])
    vcol = pl.ds(pl.multiple_of(key * vcols, 128), vcols)
    vals = vf[:, vcol].astype(BF16)

    def stacked(ref, slot, part):
        return jnp.concatenate([ref[g, slot, part].astype(F32) for g in range(groups)], axis=0)

    read_x = dot_split(mix * dots_x, vals) + stacked(rd_send, key, 0)
    read_d = dot_split(mix * dots_d, vals) + stacked(rd_send, key, 1)
    for d in range(1, n_key):
        dens[d - 1].wait_recv()
        den = den + as_column(den_recv[d])
    step = sq_norm / den
    for c in reads:
        c.wait_recv()
    for d in range(1, n_key):
        read_x = read_x + stacked(rd_recv, d, 0)
        read_d = read_d + stacked(rd_recv, d, 1)
    read = read_x + step * read_d

    sq_send[...] = as_row(jnp.sum(read * read, axis=1, keepdims=True))
    squares = []
    for d in range(1, n_key):
        c = pltpu.make_async_remote_copy(
            src_ref=sq_send,
            dst_ref=sq_recv.at[d],
            send_sem=sq_ss.at[d],
            recv_sem=sq_rs.at[d],
            device_id={"key": lax.rem(key + d, n_key)},
            device_id_type=MESH,
        )
        c.start()
        squares.append(c)
    sends += squares
    gained = (read * gain_v[...]).astype(BF16)
    w_in.wait()

    core = lax.rem(key, 2)
    chip = key // 2
    partner = key + 1 - 2 * core
    across = lax.rem(key + 2, n_key)

    def project(to_key, to_head):
        at = pl.multiple_of((to_key * n_head + to_head) * block, 128)
        return jnp.dot(gained, w_v[:, pl.ds(at, block)], preferred_element_type=F32)

    order = sorted(range(1, n_head), key=lambda o: abs(2 * o - n_head)) + [0]
    core_copy, x_copy, z_copy = {}, {}, {}
    scale = []

    def stage_a(o):
        to = lax.rem(head + o, n_head)
        core_copy[o] = []
        for part, side in enumerate((1 - chip, chip)):
            core_send[o, part] = project(2 * side + 1 - core, to).astype(BF16)
            c = pltpu.make_async_remote_copy(
                src_ref=core_send.at[o, part],
                dst_ref=core_recv.at[o, part],
                send_sem=core_ss.at[o, part],
                recv_sem=core_rs.at[o, part],
                device_id={"key": partner},
                device_id_type=MESH,
            )
            c.start()
            core_copy[o].append(c)
        for part, side in enumerate((1 - chip, chip)):
            own[o, part] = project(2 * side + core, to)

    def stage_b(o):
        core_copy[o][0].wait_recv()
        x_send[o] = (own[o, 0] + core_recv[o, 0].astype(F32)).astype(BF16)
        c = pltpu.make_async_remote_copy(
            src_ref=x_send.at[o],
            dst_ref=x_recv.at[o],
            send_sem=x_ss.at[o],
            recv_sem=x_rs.at[o],
            device_id={"key": across},
            device_id_type=MESH,
        )
        c.start()
        x_copy[o] = c
        core_copy[o][1].wait_recv()
        keep[o] = own[o, 1] + core_recv[o, 1].astype(F32)

    def stage_c(o):
        if not scale:
            total = as_column(sq_send[...])
            for d in range(1, n_key):
                squares[d - 1].wait_recv()
                total = total + as_column(sq_recv[d])
            scale.append(lax.rsqrt(total / values + 1e-06))
        x_copy[o].wait_recv()
        done = (keep[o] + x_recv[o].astype(F32)) * scale[0]
        if o == 0:
            keep[o] = done
            return
        z_send[o] = done.astype(BF16)
        c = pltpu.make_async_remote_copy(
            src_ref=z_send.at[o],
            dst_ref=z_recv.at[o],
            send_sem=z_ss.at[o],
            recv_sem=z_rs.at[o],
            device_id={"head": lax.rem(head + o, n_head)},
            device_id_type=MESH,
        )
        c.start()
        z_copy[o] = c

    for i in range(n_head + 2):
        if i < n_head:
            stage_a(order[i])
        if 0 <= i - 1 < n_head:
            stage_b(order[i - 1])
        if 0 <= i - 2 < n_head:
            stage_c(order[i - 2])
    result = keep[0]
    for o in range(1, n_head):
        z_copy[o].wait_recv()
        result = result + z_recv[o].astype(F32)
    keep[0] = result
    for s in range(seqs):
        out_ref[s] = keep[0, s * draft : (s + 1) * draft, :].astype(BF16)
    for c in sends + [c for pair in core_copy.values() for c in pair] + list(x_copy.values()) + list(z_copy.values()):
        c.wait_send()


def solution(mesh):
    n_key, n_head = mesh.shape["key"], mesh.shape["head"]
    assert n_key == 4

    def body(q, k, v, dg, wg, ridge, gain, cov, vs, w):
        seqs, _, draft, width = q.shape
        rows = cov.shape[2]
        values = vs.shape[2]
        vcols = values // n_key
        model = w.shape[2]
        block = model // (n_key * n_head)
        n = seqs * draft
        dma = pltpu.SemaphoreType.DMA
        out = pl.pallas_call(
            functools.partial(kernel, n_key, n_head),
            out_shape=jax.ShapeDtypeStruct((seqs, draft, block), BF16),
            in_specs=[pl.BlockSpec(memory_space=pl.ANY)] * 5
            + [pl.BlockSpec(memory_space=pltpu.SMEM)]
            + [pl.BlockSpec(memory_space=pl.ANY)] * 4,
            out_specs=pl.BlockSpec(memory_space=pltpu.VMEM),
            scratch_shapes=[
                pltpu.VMEM((seqs, draft, width), BF16),
                pltpu.VMEM((seqs, draft, width), BF16),
                pltpu.VMEM((seqs, draft, values), BF16),
                pltpu.VMEM((1, draft, seqs), F32),
                pltpu.VMEM((1, draft, seqs), F32),
                pltpu.VMEM(gain.shape, F32),
                pltpu.VMEM((seqs, rows, width), BF16),
                pltpu.VMEM((seqs, values, rows), BF16),
                pltpu.VMEM(w.shape[1:], BF16),
                pltpu.VMEM((n, width), F32),
                pltpu.VMEM((n, values), F32),
                pltpu.VMEM((n, width), F32),
                pltpu.VMEM((n, width), F32),
                pltpu.VMEM((n, width), F32),
                pltpu.VMEM((n, width), F32),
                pltpu.VMEM((ITERS - 1, n_key, n, rows), BF16),
                pltpu.VMEM((n // GROUP, n_key, 2, GROUP, vcols), BF16),
                pltpu.VMEM((n // GROUP, n_key, 2, GROUP, vcols), BF16),
                pltpu.VMEM((8, 128), F32),
                pltpu.VMEM((n_key, 8, 128), F32),
                pltpu.VMEM((8, 128), F32),
                pltpu.VMEM((n_key, 8, 128), F32),
                pltpu.VMEM((n_head, 2, n, block), BF16),
                pltpu.VMEM((n_head, 2, n, block), BF16),
                pltpu.VMEM((n_head, 2, n, block), F32),
                pltpu.VMEM((n_head, n, block), BF16),
                pltpu.VMEM((n_head, n, block), BF16),
                pltpu.VMEM((n_head, n, block), F32),
                pltpu.VMEM((n_head, n, block), BF16),
                pltpu.VMEM((n_head, n, block), BF16),
                dma((6,)),
                dma((seqs,)),
                dma((seqs,)),
                dma,
                dma((ITERS - 1, n_key, n // GROUP)),
                dma((ITERS - 1, n_key, n // GROUP)),
                dma((n // GROUP, n_key)),
                dma((n // GROUP, n_key)),
                dma((n_key,)),
                dma((n_key,)),
                dma((n_key,)),
                dma((n_key,)),
                dma((n_head, 2)),
                dma((n_head, 2)),
                dma((n_head,)),
                dma((n_head,)),
                dma((n_head,)),
                dma((n_head,)),
            ],
            compiler_params=pltpu.CompilerParams(collective_id=0, has_side_effects=True),
        )(
            q,
            k,
            v,
            dg.transpose(1, 2, 0),
            wg.transpose(1, 2, 0),
            ridge,
            gain,
            cov,
            vs,
            w,
        )
        return out

    placed = (
        P("batch", "head", None, None),
        P("batch", "head", None, None),
        P("batch", "head", None, None),
        P("batch", "head", None),
        P("batch", "head", None),
        P("head"),
        P("head", "key"),
        P("batch", "head", "key", None),
        P("batch", "head", None, "key"),
        P("head", "key", None),
    )
    return jax.shard_map(
        body,
        mesh=mesh,
        in_specs=placed,
        out_specs=P("batch", None, ("key", "head")),
        check_vma=False,
    )
```
